32 devices in a mesh: chaos: 2 (over core), space: 16 (over z, y, x).
Axes of the slice: x: 2, y: 2, z: 4, core: 2. Of those that a mesh axis runs over, the one named last changes fastest.
Arguments:
- rhs: float32 [64, 512, 128], P('chaos', 'space'), may hold values from -6 to 6
- start: float32 [64, 512, 128], P('chaos', 'space'), may hold values from -4 to 4
- kl_fields: float32 [13, 2, 512, 128], P(None, None, 'space'), may hold values from -0.07 to 4
- coupling: float32 [13, 64, 64], replicated, may hold values from -1 to 1
- order: int32 [64], replicated, may hold values from 0 to 31, as said below
Outputs:
- solution: float32 [64, 512, 128], P('chaos', 'space')
The draws below stay inside these ranges and needn't reach their ends.
Inputs may be any that keep to these rules, and one draw needn't show every extreme that they name: `order`: within each aligned run of 32 entries every section 0 .. 31 appears exactly once.
All inputs are finite; a program needn't handle non-finite values.
Results may differ from the reference program's by a relative error of at most 0.0001.
Values sent between devices are 32-bit elements; how exact they have to be, the bound alone decides.
No kernel may reach another device: no remote copies, remote signals or barrier semaphores. Data moves between devices by JAX's collectives and lax.ppermute only.
A program may use at most 64 MiB of HBM per device.

```python
import jax
import jax.numpy as jnp
from jax import lax

COEFFS = 64
KL_TERMS = 12
INNER = 3
SECTIONS = 3
ACROSS = 128
ROWS = 512
BLOCKS_DEV = 32
N_CHAOS = 2


def draw_kl_fields(key, part):
    first_key, second_key = jax.random.split(jax.random.fold_in(key, 11), 2)
    mean_part = jnp.exp(jax.random.uniform(first_key, (1, 2, ROWS, ACROSS), jnp.float32, 0.0, jnp.log(4.0)))
    modes = jax.random.uniform(second_key, (KL_TERMS, 2, ROWS, ACROSS), jnp.float32, -0.07, 0.07)
    return jnp.concatenate([mean_part, modes], axis=0).astype(jnp.float32)


def draw_coupling(key, part):
    first_key, second_key = jax.random.split(jax.random.fold_in(key, 23), 2)
    values = jax.random.uniform(first_key, (KL_TERMS, COEFFS, COEFFS), jnp.float32, -1.0, 1.0)
    values = 0.5 * (values + jnp.transpose(values, (0, 2, 1)))
    keep_mask = jax.random.randint(second_key, (KL_TERMS, COEFFS, COEFFS), 0, 4) == 0
    keep_mask = keep_mask | jnp.transpose(keep_mask, (0, 2, 1))
    identity = jnp.eye(COEFFS, dtype=jnp.float32)
    keep_mask = keep_mask | (identity[None] > 0.5)
    modes = jnp.where(keep_mask, values, 0.0)
    return jnp.concatenate([identity[None], modes], axis=0).astype(jnp.float32)


def draw_order(key, part):
    group_count = COEFFS // BLOCKS_DEV
    group_keys = jax.random.split(jax.random.fold_in(key, 37), group_count)
    perms = jax.vmap(lambda single_key: jax.random.permutation(single_key, BLOCKS_DEV))(group_keys)
    return perms.reshape(COEFFS).astype(jnp.int32)


def block_scale(stream_key, dims, cuts, smallest, top_value):
    def one(dim, parts):
        draws = jax.random.uniform(jax.random.fold_in(jax.random.fold_in(stream_key, 6), dim), (parts,), jnp.float32, smallest / len(cuts), top_value / len(cuts))
        return jnp.repeat(jnp.exp(draws), dims[dim] // parts).reshape((-1,) + (1,) * (len(dims) - dim - 1))

    loudness = one(*cuts[0])
    for cut in cuts[1:]:
        loudness = loudness * one(*cut)
    return loudness


def noise(stream_key, dims, spread, most, cuts=(), kind=jnp.bfloat16):
    loudness = block_scale(stream_key, dims, cuts, -0.22, 0.18) if cuts else 1.0
    values = jax.random.normal(stream_key, dims, jnp.float32) * spread * loudness
    return jnp.minimum(jnp.maximum(values, -most), most).astype(kind)


def setup_inputs(seed: int = 0) -> dict:
    seeds = jax.random.split(jax.random.key(seed), 6)
    return {
        "rhs": noise(seeds[0], (COEFFS, ROWS, ACROSS), 1.0, 6.0, ((0, 2), (1, 16)), jnp.float32),
        "start": noise(seeds[1], (COEFFS, ROWS, ACROSS), 0.5, 4.0, ((0, 2), (1, 16)), jnp.float32),
        "kl_fields": draw_kl_fields(jax.random.fold_in(seeds[5], 71), 0),
        "coupling": draw_coupling(jax.random.fold_in(seeds[5], 71), 0),
        "order": draw_order(jax.random.fold_in(seeds[5], 71), 0),
    }


HIGHEST = lax.Precision.HIGHEST


def divergence(fields, coef_x, coef_y):
    grad_x = fields - jnp.concatenate([jnp.zeros_like(fields[:, :1, :]), fields[:, :-1, :]], axis=1)
    flux_x = jnp.sum(coef_x * grad_x, axis=0)
    result = flux_x - jnp.concatenate([flux_x[1:], jnp.zeros_like(flux_x[:1])], axis=0)
    grad_y = fields - jnp.concatenate([jnp.zeros_like(fields[:, :, :1]), fields[:, :, :-1]], axis=2)
    flux_y = jnp.sum(coef_y * grad_y, axis=0)
    return result + flux_y - jnp.concatenate([flux_y[:, 1:], jnp.zeros_like(flux_y[:, :1])], axis=1)


def conjugate(residual, coef_x, coef_y, diagonal):
    precond = residual / diagonal
    search = precond
    update = jnp.zeros_like(residual)
    norm_now = jnp.sum(residual * precond)
    for sweep in range(INNER):
        image = divergence(search[None], coef_x, coef_y)
        step_len = norm_now / jnp.sum(search * image)
        update = update + step_len * search
        residual = residual - step_len * image
        if sweep + 1 < INNER:
            precond = residual / diagonal
            norm_next = jnp.sum(residual * precond)
            search = precond + (norm_next / norm_now) * search
            norm_now = norm_next
    return update


def reference(rhs, start, kl_fields, coupling, order):
    coef_x = kl_fields[:, 0]
    coef_y = kl_fields[:, 1]
    mean_x = coef_x[0]
    mean_y = coef_y[0]
    diagonal = mean_x + jnp.concatenate([mean_x[1:], jnp.zeros_like(mean_x[:1])], axis=0)
    diagonal = diagonal + mean_y + jnp.concatenate([mean_y[:, 1:], jnp.zeros_like(mean_y[:, :1])], axis=1)
    flat_blocks = start.reshape(COEFFS, ROWS * ACROSS)
    groups = order.reshape(N_CHAOS, BLOCKS_DEV)
    slot_ids = jnp.arange(BLOCKS_DEV, dtype=jnp.int32)
    for section_num in range(SECTIONS):
        section_slots = jnp.sum(jnp.where(groups == section_num, slot_ids[None, :], 0), axis=1).astype(jnp.int32)
        targets = (jnp.arange(N_CHAOS, dtype=jnp.int32) * BLOCKS_DEV + section_slots).astype(jnp.int32)

        def solve_one(target, current=flat_blocks):
            coupling_row = lax.dynamic_index_in_dim(coupling, target, 1, keepdims=False)
            fields = jnp.dot(coupling_row, current, precision=HIGHEST).reshape(KL_TERMS + 1, ROWS, ACROSS)
            coupled = divergence(fields, coef_x, coef_y)
            own_rhs = lax.dynamic_index_in_dim(rhs, target, 0, keepdims=False)
            weights = lax.dynamic_index_in_dim(coupling_row, target, 1, keepdims=False)
            block_x = jnp.tensordot(weights, coef_x, axes=1, precision=HIGHEST)[None]
            block_y = jnp.tensordot(weights, coef_y, axes=1, precision=HIGHEST)[None]
            return conjugate(own_rhs - coupled, block_x, block_y, diagonal).reshape(ROWS * ACROSS)

        updates = lax.map(solve_one, targets)
        flat_blocks = flat_blocks.at[targets].add(updates)
    return flat_blocks.reshape(COEFFS, ROWS, ACROSS)
```

```python
import jax
import jax.numpy as jnp
from jax import lax
from jax.experimental import pallas as pl
from jax.experimental.pallas import tpu as pltpu
from jax.sharding import PartitionSpec as P

INNER = 3
SECTIONS = 3
HALO = 10
EDGE = 16
TERM_PAD = 16
SCALE = 2.0 ** -16
HIGHEST = lax.Precision.HIGHEST
F32 = jnp.float32


def round_up(value, step):
    return (value + step - 1) // step * step


def dot(left, right, contract):
    return lax.dot_general(left, right, (contract, ((), ())), precision=HIGHEST, preferred_element_type=F32)


def slots_of(order_ref, first, count):
    found = [jnp.int32(0)] * SECTIONS
    for place in range(count):
        section = order_ref[first + place]
        found = [jnp.where(section == s, jnp.int32(place), found[s]) for s in range(SECTIONS)]
    return found


def lane_masks(rows, cols):
    lanes = lax.broadcasted_iota(jnp.int32, (rows, cols), 1)
    return (lanes > 0).astype(F32), (lanes < cols - 1).astype(F32)


def apply_edges(field, edge_x, edge_y, masks):
    rows, cols = field.shape
    flux_x = edge_x * (field - pltpu.roll(field, 1, 0))
    flux_y = edge_y * (field - masks[0] * pltpu.roll(field, 1, 1))
    return flux_x - pltpu.roll(flux_x, rows - 1, 0) + flux_y - masks[1] * pltpu.roll(flux_y, cols - 1, 1)


def base_kernel(dims, order_ref, coupling_ref, start_ref, rhs_ref, kl_ref, pay_ref, pairs_ref, rows_ref, fields_ref):
    groups, count, rows, cols, terms, targets = dims
    rank = lax.axis_index("chaos")
    tall = TERM_PAD * targets
    slots = [slots_of(order_ref, g * count, count) for g in range(groups)]
    places = [g * count + slots[g][s] for s in range(SECTIONS) for g in range(groups)]
    rows_ref[...] = jnp.zeros_like(rows_ref)
    for t in range(targets):
        for k in range(terms):
            rows_ref[t * TERM_PAD + k : t * TERM_PAD + k + 1, :] = coupling_ref[k, pl.ds(places[t], 1), :]
    every = rows_ref[...]
    hot_rows = pairs_ref.shape[0]
    hot_row = lax.broadcasted_iota(jnp.int32, (hot_rows, every.shape[1]), 0)
    hot_col = lax.broadcasted_iota(jnp.int32, (hot_rows, every.shape[1]), 1)
    wanted = jnp.full((hot_rows, every.shape[1]), -1, jnp.int32)
    for t in range(targets):
        wanted = jnp.where(hot_row == t, places[t], wanted)
    pairs_ref[...] = dot((hot_col == wanted).astype(F32), every, ((1,), (1,)))
    own = every[:tall, :count]
    for g in range(1, groups):
        own = jnp.where(rank == g, every[:tall, g * count : (g + 1) * count], own)
    for r in range(rows):
        line = start_ref[pl.ds(r, count, stride=rows), :]
        fields_ref[pl.ds(r, tall, stride=rows), :] = dot(own, line, ((1,), (0,)))
    pay_ref[targets * rows : targets * rows + tall, :] = fields_ref[pl.ds(0, tall, stride=rows), :]
    pay_ref[targets * rows + tall :, :] = fields_ref[pl.ds(rows - 1, tall, stride=rows), :]
    masks = lane_masks(rows, cols)
    inner = (lax.broadcasted_iota(jnp.int32, (rows, cols), 0) > 0).astype(F32)
    for t in range(targets):
        flux_x = jnp.zeros((rows, cols), F32)
        flux_y = jnp.zeros((rows, cols), F32)
        for k in range(terms):
            first = (t * TERM_PAD + k) * rows
            field = fields_ref[first : first + rows, :]
            edge_x = kl_ref[2 * k * rows : (2 * k + 1) * rows, :]
            edge_y = kl_ref[(2 * k + 1) * rows : (2 * k + 2) * rows, :]
            flux_x = flux_x + edge_x * (field - pltpu.roll(field, 1, 0))
            flux_y = flux_y + edge_y * (field - masks[0] * pltpu.roll(field, 1, 1))
        flux_x = flux_x * inner
        coupled = flux_x - pltpu.roll(flux_x, rows - 1, 0) + flux_y - masks[1] * pltpu.roll(flux_y, cols - 1, 1)
        section, group = divmod(t, groups)
        load = rhs_ref[slots[group][section]]
        pay_ref[t * rows : (t + 1) * rows, :] = jnp.where(rank == group, load, 0.0) - coupled


def pack_kernel(dims, pay_ref, other_ref, kl_ref, full_ref, halo_ref):
    groups, count, rows, cols, terms, targets = dims
    tall = TERM_PAD * targets
    full_ref[...] = pay_ref[...] + other_ref[...]
    upward = lax.axis_index("chaos") % 2 == 0

    def fill(first, line):
        for f in range(2 * terms):
            halo_ref[f * HALO : (f + 1) * HALO, :] = kl_ref[f * rows + first : f * rows + first + HALO, :]
        for t in range(targets):
            put = (2 * terms + t) * HALO
            halo_ref[put : put + HALO, :] = full_ref[t * rows + first : t * rows + first + HALO, :]
        put = (2 * terms + targets) * HALO
        halo_ref[put : put + tall, :] = full_ref[line : line + tall, :]

    @pl.when(upward)
    def _():
        fill(rows - HALO, targets * rows + tall)

    @pl.when(jnp.logical_not(upward))
    def _():
        fill(0, targets * rows)


def krylov(residual, edges, scale_in, masks):
    first = scale_in[0] * residual
    basis = [first]
    for _ in range(INNER - 1):
        last = basis[-1]
        basis.append(scale_in[1] * apply_edges(last, *edges, masks) - SCALE * last)
    return basis


def moments_of(basis, edges, scale_in, diagonal, masks, rows):
    last = basis[-1]
    basis = basis + [scale_in[1] * apply_edges(last, *edges, masks) - SCALE * last]
    mine = slice(EDGE, EDGE + rows)
    weighted = diagonal[mine]
    out = []
    for m in range(2 * INNER):
        out.append(jnp.sum(basis[m // 2][mine] * basis[m - m // 2][mine] * weighted, axis=0, keepdims=True))
    return out


def coefficients(mu):
    inv = 1.0 / SCALE

    def inner(left, right, extra):
        total = None
        for i, a in enumerate(left):
            for j, b in enumerate(right):
                term = a * b * (mu[i + j] if not extra else mu[i + j + 1] * inv + mu[i + j])
                total = term if total is None else total + term
        return total

    one = jnp.ones_like(mu[0])
    precond = [one]
    search = [one]
    norm = mu[0]
    update = [jnp.zeros_like(one)] * INNER
    for sweep in range(INNER):
        step = norm / inner(search, search, True)
        update = [u + step * search[i] if i < len(search) else u for i, u in enumerate(update)]
        if sweep + 1 == INNER:
            break
        image = [jnp.zeros_like(one)] * (len(search) + 1)
        for i, c in enumerate(search):
            image[i] = image[i] + c
            image[i + 1] = image[i + 1] + c * inv
        precond = [(precond[i] if i < len(precond) else 0.0) - step * c for i, c in enumerate(image)]
        following = inner(precond, precond, False)
        ratio = following / norm
        search = [p + ratio * search[i] if i < len(search) else p for i, p in enumerate(precond)]
        norm = following
    return update


def combine(basis, weights):
    total = weights[0] * basis[0]
    for v, w in zip(basis[1:], weights[1:]):
        total = total + w * v
    return total


def scatter(moments_ref, lines):
    moments_ref[...] = jnp.zeros_like(moments_ref)
    for i, line in enumerate(lines):
        for d in range(moments_ref.shape[0]):
            moments_ref[d, i : i + 1, :] = line


def gather(arrived_ref):
    total = jnp.sum(arrived_ref[...], axis=0)
    cols = total.shape[1]
    return dot(total, jnp.ones((cols, cols), F32), ((1,), (0,)))


def first_kernel(dims, pairs_ref, full_ref, kl_ref, got_ref, swapped_ref,
                 moments_ref, basis_ref, resid_ref, edges_ref, diag_ref, ext_ref, line_ref):
    groups, count, rows, cols, terms, targets = dims
    tall = TERM_PAD * targets
    size = rows + 2 * EDGE
    rank = lax.axis_index("chaos")
    place = lax.axis_index("space")
    last = lax.axis_size("space") - 1
    lines_at = (2 * terms + targets) * HALO
    ext_ref[...] = jnp.zeros_like(ext_ref)

    def fill(lower, upper):
        for f in range(2 * terms + targets):
            ext_ref[f, EDGE - HALO : EDGE, :] = lower[f * HALO : (f + 1) * HALO, :]
            ext_ref[f, EDGE + rows : EDGE + rows + HALO, :] = upper[f * HALO : (f + 1) * HALO, :]
        line_ref[0] = lower[lines_at : lines_at + tall, :]
        line_ref[1] = upper[lines_at : lines_at + tall, :]

    @pl.when(rank % 2 == 0)
    def _():
        fill(got_ref, swapped_ref)

    @pl.when(rank % 2 == 1)
    def _():
        fill(swapped_ref, got_ref)

    for f in range(2 * terms):
        ext_ref[f, EDGE : EDGE + rows, :] = kl_ref[f * rows : (f + 1) * rows, :]
    for t in range(targets):
        ext_ref[2 * terms + t, EDGE : EDGE + rows, :] = full_ref[t * rows : (t + 1) * rows, :]
    bottom = targets * rows
    top = bottom + tall
    for edge, below, above in (
        (EDGE, line_ref[0], full_ref[bottom : bottom + tall, :]),
        (EDGE + rows, full_ref[top : top + tall, :], line_ref[1]),
    ):
        jump = above - below
        stiff = [ext_ref[2 * k, edge : edge + 1, :] for k in range(terms)]
        for t in range(targets):
            flux = stiff[0] * jump[t * TERM_PAD : t * TERM_PAD + 1]
            for k in range(1, terms):
                flux = flux + stiff[k] * jump[t * TERM_PAD + k : t * TERM_PAD + k + 1]
            ext_ref[2 * terms + t, edge : edge + 1, :] = ext_ref[2 * terms + t, edge : edge + 1, :] - flux
            ext_ref[2 * terms + t, edge - 1 : edge, :] = ext_ref[2 * terms + t, edge - 1 : edge, :] + flux

    masks = lane_masks(size, cols)
    mean_x = ext_ref[0]
    mean_y = ext_ref[1]
    diagonal = mean_x + pltpu.roll(mean_x, size - 1, 0) + mean_y + masks[1] * pltpu.roll(mean_y, cols - 1, 1)
    row = lax.broadcasted_iota(jnp.int32, (size, cols), 0)
    low = jnp.where(place == 0, EDGE, EDGE - HALO + 1)
    high = jnp.where(place == last, EDGE + rows, EDGE + rows + HALO - 1)
    inverse = jnp.where((row >= low) & (row < high), 1.0 / diagonal, 0.0)
    diag_ref[0] = diagonal
    diag_ref[1] = inverse
    scale_in = (inverse, SCALE * inverse)

    def coef(t, j):
        edge_x = pairs_ref[j, t * TERM_PAD] * ext_ref[0]
        edge_y = pairs_ref[j, t * TERM_PAD] * ext_ref[1]
        for k in range(1, terms):
            factor = pairs_ref[j, t * TERM_PAD + k]
            edge_x = edge_x + factor * ext_ref[2 * k]
            edge_y = edge_y + factor * ext_ref[2 * k + 1]
        return edge_x, edge_y

    lines = []
    for g in range(groups):
        edges = coef(g, g)
        basis = krylov(ext_ref[2 * terms + g], edges, scale_in, masks)
        for i, v in enumerate(basis):
            basis_ref[g * INNER + i] = v
        lines += moments_of(basis, edges, scale_in, diagonal, masks, rows)
    scatter(moments_ref, lines)

    def keep(at, t, j):
        edge_x, edge_y = coef(t, j)
        edges_ref[2 * at] = edge_x
        edges_ref[2 * at + 1] = edge_y

    at = 0
    for g in range(groups):
        resid_ref[g] = ext_ref[2 * terms + groups + g]
        keep(at, groups + g, groups + g)
        at += 1
        for j in range(groups):
            keep(at, groups + g, j)
            at += 1
    final = 2 * groups + rank
    resid_ref[groups] = ext_ref[2 * terms + final]
    keep(at, final, final)
    at += 1
    for j in range(2 * groups):
        keep(at, final, j)
        at += 1


def second_kernel(dims, arrived_ref, basis_ref, resid_ref, edges_ref, diag_ref, moments_ref, next_ref, update_ref):
    groups, count, rows, cols, terms, targets = dims
    size = rows + 2 * EDGE
    masks = lane_masks(size, cols)
    total = gather(arrived_ref)
    updates = []
    for g in range(groups):
        mu = [total[g * 2 * INNER + m : g * 2 * INNER + m + 1] for m in range(2 * INNER)]
        updates.append(combine([basis_ref[g * INNER + i] for i in range(INNER)], coefficients(mu)))
        update_ref[g] = updates[g]
    scale_in = (diag_ref[1], SCALE * diag_ref[1])
    lines = []
    at = 0
    for g in range(groups):
        edges = (edges_ref[2 * at], edges_ref[2 * at + 1])
        at += 1
        residual = resid_ref[g]
        for j in range(groups):
            residual = residual - apply_edges(updates[j], edges_ref[2 * at], edges_ref[2 * at + 1], masks)
            at += 1
        basis = krylov(residual, edges, scale_in, masks)
        for i, v in enumerate(basis):
            next_ref[g * INNER + i] = v
        lines += moments_of(basis, edges, scale_in, diag_ref[0], masks, rows)
    scatter(moments_ref, lines)


def third_kernel(dims, arrived_ref, basis_ref, resid_ref, edges_ref, diag_ref, before_ref, moments_ref, next_ref, update_ref):
    groups, count, rows, cols, terms, targets = dims
    size = rows + 2 * EDGE
    masks = lane_masks(size, cols)
    total = gather(arrived_ref)
    updates = [before_ref[g] for g in range(groups)]
    for g in range(groups):
        mu = [total[g * 2 * INNER + m : g * 2 * INNER + m + 1] for m in range(2 * INNER)]
        updates.append(combine([basis_ref[g * INNER + i] for i in range(INNER)], coefficients(mu)))
        update_ref[g] = updates[-1]
    scale_in = (diag_ref[1], SCALE * diag_ref[1])
    at = groups * (1 + groups)
    edges = (edges_ref[2 * at], edges_ref[2 * at + 1])
    at += 1
    residual = resid_ref[groups]
    for update in updates:
        residual = residual - apply_edges(update, edges_ref[2 * at], edges_ref[2 * at + 1], masks)
        at += 1
    basis = krylov(residual, edges, scale_in, masks)
    for i, v in enumerate(basis):
        next_ref[i] = v
    scatter(moments_ref, moments_of(basis, edges, scale_in, diag_ref[0], masks, rows))


def last_kernel(dims, order_ref, arrived_ref, basis_ref, first_ref, second_ref, start_ref, out_ref):
    groups, count, rows, cols, terms, targets = dims
    rank = lax.axis_index("chaos")
    total = gather(arrived_ref)
    mu = [total[m : m + 1] for m in range(2 * INNER)]
    mine = slice(EDGE, EDGE + rows)
    final = combine([basis_ref[i][mine] for i in range(INNER)], coefficients(mu))
    slots = slots_of(order_ref, rank * count, count)
    out_ref[...] = start_ref[...]
    out_ref[slots[0]] = out_ref[slots[0]] + first_ref[rank, mine, :]
    out_ref[slots[1]] = out_ref[slots[1]] + second_ref[rank, mine, :]
    out_ref[slots[2]] = out_ref[slots[2]] + final


def on_device(rhs, start, kl_fields, coupling, order):
    count, rows, cols = start.shape
    terms = kl_fields.shape[0]
    groups = lax.axis_size("chaos")
    spaces = lax.axis_size("space")
    targets = SECTIONS * groups
    dims = (groups, count, rows, cols, terms, targets)
    tall = TERM_PAD * targets
    size = rows + 2 * EDGE
    wide = round_up(tall, 128)
    vmem = pl.BlockSpec(memory_space=pltpu.VMEM)
    smem = pl.BlockSpec(memory_space=pltpu.SMEM)

    def call(body, specs, outs, scratch=()):
        return pl.pallas_call(
            lambda *refs: body(dims, *refs),
            out_shape=[jax.ShapeDtypeStruct(s, F32) for s in outs],
            in_specs=specs,
            out_specs=[vmem] * len(outs),
            scratch_shapes=[pltpu.VMEM(s, F32) for s in scratch],
            name=body.__name__,
        )

    flat_start = start.reshape(count * rows, cols)
    flat_kl = kl_fields.reshape(2 * terms * rows, cols)
    pay_rows = targets * rows + 2 * tall
    pay, pairs = call(
        base_kernel, [smem, vmem, vmem, vmem, vmem],
        [(pay_rows, cols), (round_up(targets, 8), wide)],
        [(wide, coupling.shape[1]), (tall * rows, cols)],
    )(order, coupling, flat_start, rhs, flat_kl)

    def swap(array, bit):
        return lax.ppermute(array, "chaos", [(i, i ^ bit) for i in range(groups)])

    bit = groups // 2
    while bit > 1:
        pay = pay + swap(pay, bit)
        bit //= 2
    other = swap(pay, 1)
    halo_rows = round_up((2 * terms + targets) * HALO + tall, 8)
    full, halo = call(
        pack_kernel, [vmem] * 3, [(pay_rows, cols), (halo_rows, cols)]
    )(pay, other, flat_kl)
    pairs_list = []
    for c in range(groups):
        step = 1 if c % 2 == 0 else -1
        for i in range(spaces):
            if 0 <= i + step < spaces:
                pairs_list.append((c * spaces + i, c * spaces + i + step))
    got = lax.ppermute(halo, ("chaos", "space"), pairs_list)
    swapped = swap(got, 1)
    couples = groups * (1 + groups) + 1 + 2 * groups
    moment_rows = round_up(groups * 2 * INNER, 8)
    moments, basis, resid, edges, diag = call(
        first_kernel, [smem, vmem, vmem, vmem, vmem],
        [(spaces, moment_rows, cols), (groups * INNER, size, cols), (groups + 1, size, cols),
         (2 * couples, size, cols), (2, size, cols)],
        [(2 * terms + targets, size, cols), (2, tall, cols)],
    )(pairs, full, flat_kl, got, swapped)

    def share(array):
        return lax.all_to_all(array, "space", 0, 0, tiled=True)

    moments, basis, update0 = call(
        second_kernel, [vmem] * 5,
        [(spaces, moment_rows, cols), (groups * INNER, size, cols), (groups, size, cols)],
    )(share(moments), basis, resid, edges, diag)
    moments, basis, update1 = call(
        third_kernel, [vmem] * 6,
        [(spaces, 8, cols), (INNER, size, cols), (groups, size, cols)],
    )(share(moments), basis, resid, edges, diag, update0)
    (out,) = call(
        last_kernel, [smem] + [vmem] * 5, [(count, rows, cols)]
    )(order, share(moments), basis, update0, update1, start)
    return out


def solution(mesh):
    return jax.shard_map(
        on_device,
        mesh=mesh,
        in_specs=(
            P("chaos", "space", None),
            P("chaos", "space", None),
            P(None, None, "space", None),
            P(),
            P(),
        ),
        out_specs=P("chaos", "space", None),
        check_vma=False,
    )
```

```python
import jax
import jax.numpy as jnp
from jax import lax
from jax.experimental import pallas as pl
from jax.experimental.pallas import tpu as pltpu
from jax.sharding import PartitionSpec as P

INNER = 3
SECTIONS = 3
HALO = 10
EDGE = 16
TERM_PAD = 16
SCALE = 2.0 ** -16
HIGHEST = lax.Precision.HIGHEST
F32 = jnp.float32


def round_up(value, step):
    return (value + step - 1) // step * step


def dot(left, right, contract):
    return lax.dot_general(left, right, (contract, ((), ())), precision=HIGHEST, preferred_element_type=F32)


def slots_of(order_ref, first, count):
    found = [jnp.int32(0)] * SECTIONS
    for place in range(count):
        section = order_ref[first + place]
        found = [jnp.where(section == s, jnp.int32(place), found[s]) for s in range(SECTIONS)]
    return found


def lane_masks(rows, cols):
    lanes = lax.broadcasted_iota(jnp.int32, (rows, cols), 1)
    return (lanes > 0).astype(F32), (lanes < cols - 1).astype(F32)


def apply_edges(field, edge_x, edge_y, masks):
    rows, cols = field.shape
    flux_x = edge_x * (field - pltpu.roll(field, 1, 0))
    flux_y = edge_y * (field - masks[0] * pltpu.roll(field, 1, 1))
    return flux_x - pltpu.roll(flux_x, rows - 1, 0) + flux_y - masks[1] * pltpu.roll(flux_y, cols - 1, 1)


def base_kernel(dims, order_ref, coupling_ref, start_ref, rhs_ref, kl_ref, pay_ref, pairs_ref, rows_ref, fields_ref):
    groups, count, rows, cols, terms, targets = dims
    rank = lax.axis_index("chaos")
    tall = TERM_PAD * targets
    slots = [slots_of(order_ref, g * count, count) for g in range(groups)]
    places = [g * count + slots[g][s] for s in range(SECTIONS) for g in range(groups)]
    rows_ref[...] = jnp.zeros_like(rows_ref)
    for t in range(targets):
        for k in range(terms):
            rows_ref[t * TERM_PAD + k : t * TERM_PAD + k + 1, :] = coupling_ref[k, pl.ds(places[t], 1), :]
    every = rows_ref[...]
    hot_rows = pairs_ref.shape[0]
    hot_row = lax.broadcasted_iota(jnp.int32, (hot_rows, every.shape[1]), 0)
    hot_col = lax.broadcasted_iota(jnp.int32, (hot_rows, every.shape[1]), 1)
    wanted = jnp.full((hot_rows, every.shape[1]), -1, jnp.int32)
    for t in range(targets):
        wanted = jnp.where(hot_row == t, places[t], wanted)
    pairs_ref[...] = dot((hot_col == wanted).astype(F32), every, ((1,), (1,)))
    own = every[:tall, :count]
    for g in range(1, groups):
        own = jnp.where(rank == g, every[:tall, g * count : (g + 1) * count], own)
    for r in range(rows):
        line = start_ref[pl.ds(r, count, stride=rows), :]
        fields_ref[pl.ds(r, tall, stride=rows), :] = dot(own, line, ((1,), (0,)))
    pay_ref[targets * rows : targets * rows + tall, :] = fields_ref[pl.ds(0, tall, stride=rows), :]
    pay_ref[targets * rows + tall :, :] = fields_ref[pl.ds(rows - 1, tall, stride=rows), :]
    masks = lane_masks(rows, cols)
    inner = (lax.broadcasted_iota(jnp.int32, (rows, cols), 0) > 0).astype(F32)
    for t in range(targets):
        flux_x = jnp.zeros((rows, cols), F32)
        flux_y = jnp.zeros((rows, cols), F32)
        for k in range(terms):
            first = (t * TERM_PAD + k) * rows
            field = fields_ref[first : first + rows, :]
            edge_x = kl_ref[2 * k * rows : (2 * k + 1) * rows, :]
            edge_y = kl_ref[(2 * k + 1) * rows : (2 * k + 2) * rows, :]
            flux_x = flux_x + edge_x * (field - pltpu.roll(field, 1, 0))
            flux_y = flux_y + edge_y * (field - masks[0] * pltpu.roll(field, 1, 1))
        flux_x = flux_x * inner
        coupled = flux_x - pltpu.roll(flux_x, rows - 1, 0) + flux_y - masks[1] * pltpu.roll(flux_y, cols - 1, 1)
        section, group = divmod(t, groups)
        load = rhs_ref[slots[group][section]]
        pay_ref[t * rows : (t + 1) * rows, :] = jnp.where(rank == group, load, 0.0) - coupled


def pack_kernel(dims, pay_ref, other_ref, kl_ref, full_ref, halo_ref):
    groups, count, rows, cols, terms, targets = dims
    tall = TERM_PAD * targets
    full_ref[...] = pay_ref[...] + other_ref[...]
    upward = lax.axis_index("chaos") % 2 == 0

    def fill(first, line):
        for f in range(2 * terms):
            halo_ref[f * HALO : (f + 1) * HALO, :] = kl_ref[f * rows + first : f * rows + first + HALO, :]
        for t in range(targets):
            put = (2 * terms + t) * HALO
            halo_ref[put : put + HALO, :] = full_ref[t * rows + first : t * rows + first + HALO, :]
        put = (2 * terms + targets) * HALO
        halo_ref[put : put + tall, :] = full_ref[line : line + tall, :]

    @pl.when(upward)
    def _():
        fill(rows - HALO, targets * rows + tall)

    @pl.when(jnp.logical_not(upward))
    def _():
        fill(0, targets * rows)


def krylov(residual, edges, scale_in, masks):
    first = scale_in[0] * residual
    basis = [first]
    for _ in range(INNER - 1):
        last = basis[-1]
        basis.append(scale_in[1] * apply_edges(last, *edges, masks) - SCALE * last)
    return basis


def moments_of(basis, edges, scale_in, diagonal, masks, rows):
    last = basis[-1]
    basis = basis + [scale_in[1] * apply_edges(last, *edges, masks) - SCALE * last]
    mine = slice(EDGE, EDGE + rows)
    weighted = diagonal[mine]
    out = []
    for m in range(2 * INNER):
        out.append(jnp.sum(basis[m // 2][mine] * basis[m - m // 2][mine] * weighted, axis=0, keepdims=True))
    return out


def coefficients(mu):
    inv = 1.0 / SCALE

    def inner(left, right, extra):
        total = None
        for i, a in enumerate(left):
            for j, b in enumerate(right):
                term = a * b * (mu[i + j] if not extra else mu[i + j + 1] * inv + mu[i + j])
                total = term if total is None else total + term
        return total

    one = jnp.ones_like(mu[0])
    precond = [one]
    search = [one]
    norm = mu[0]
    update = [jnp.zeros_like(one)] * INNER
    for sweep in range(INNER):
        step = norm / inner(search, search, True)
        update = [u + step * search[i] if i < len(search) else u for i, u in enumerate(update)]
        if sweep + 1 == INNER:
            break
        image = [jnp.zeros_like(one)] * (len(search) + 1)
        for i, c in enumerate(search):
            image[i] = image[i] + c
            image[i + 1] = image[i + 1] + c * inv
        precond = [(precond[i] if i < len(precond) else 0.0) - step * c for i, c in enumerate(image)]
        following = inner(precond, precond, False)
        ratio = following / norm
        search = [p + ratio * search[i] if i < len(search) else p for i, p in enumerate(precond)]
        norm = following
    return update


def combine(basis, weights):
    total = weights[0] * basis[0]
    for v, w in zip(basis[1:], weights[1:]):
        total = total + w * v
    return total


def scatter(moments_ref, lines):
    moments_ref[...] = jnp.zeros_like(moments_ref)
    for i, line in enumerate(lines):
        for d in range(moments_ref.shape[0]):
            moments_ref[d, i : i + 1, :] = line


def gather(arrived_ref):
    total = jnp.sum(arrived_ref[...], axis=0)
    cols = total.shape[1]
    return dot(total, jnp.ones((cols, cols), F32), ((1,), (0,)))


def first_kernel(dims, pairs_ref, full_ref, kl_ref, got_ref, swapped_ref,
                 moments_ref, basis_ref, resid_ref, edges_ref, diag_ref, ext_ref, line_ref):
    groups, count, rows, cols, terms, targets = dims
    tall = TERM_PAD * targets
    size = rows + 2 * EDGE
    rank = lax.axis_index("chaos")
    place = lax.axis_index("space")
    last = lax.axis_size("space") - 1
    lines_at = (2 * terms + targets) * HALO
    ext_ref[...] = jnp.zeros_like(ext_ref)

    def fill(lower, upper):
        for f in range(2 * terms + targets):
            ext_ref[f, EDGE - HALO : EDGE, :] = lower[f * HALO : (f + 1) * HALO, :]
            ext_ref[f, EDGE + rows : EDGE + rows + HALO, :] = upper[f * HALO : (f + 1) * HALO, :]
        line_ref[0] = lower[lines_at : lines_at + tall, :]
        line_ref[1] = upper[lines_at : lines_at + tall, :]

    @pl.when(rank % 2 == 0)
    def _():
        fill(got_ref, swapped_ref)

    @pl.when(rank % 2 == 1)
    def _():
        fill(swapped_ref, got_ref)

    for f in range(2 * terms):
        ext_ref[f, EDGE : EDGE + rows, :] = kl_ref[f * rows : (f + 1) * rows, :]
    for t in range(targets):
        ext_ref[2 * terms + t, EDGE : EDGE + rows, :] = full_ref[t * rows : (t + 1) * rows, :]
    bottom = targets * rows
    top = bottom + tall
    for edge, below, above in (
        (EDGE, line_ref[0], full_ref[bottom : bottom + tall, :]),
        (EDGE + rows, full_ref[top : top + tall, :], line_ref[1]),
    ):
        jump = above - below
        stiff = [ext_ref[2 * k, edge : edge + 1, :] for k in range(terms)]
        for t in range(targets):
            flux = stiff[0] * jump[t * TERM_PAD : t * TERM_PAD + 1]
            for k in range(1, terms):
                flux = flux + stiff[k] * jump[t * TERM_PAD + k : t * TERM_PAD + k + 1]
            ext_ref[2 * terms + t, edge : edge + 1, :] = ext_ref[2 * terms + t, edge : edge + 1, :] - flux
            ext_ref[2 * terms + t, edge - 1 : edge, :] = ext_ref[2 * terms + t, edge - 1 : edge, :] + flux

    masks = lane_masks(size, cols)
    mean_x = ext_ref[0]
    mean_y = ext_ref[1]
    diagonal = mean_x + pltpu.roll(mean_x, size - 1, 0) + mean_y + masks[1] * pltpu.roll(mean_y, cols - 1, 1)
    row = lax.broadcasted_iota(jnp.int32, (size, cols), 0)
    low = jnp.where(place == 0, EDGE, EDGE - HALO + 1)
    high = jnp.where(place == last, EDGE + rows, EDGE + rows + HALO - 1)
    inverse = jnp.where((row >= low) & (row < high), 1.0 / diagonal, 0.0)
    diag_ref[0] = diagonal
    diag_ref[1] = inverse
    scale_in = (inverse, SCALE * inverse)

    def coef(t, j):
        edge_x = pairs_ref[j, t * TERM_PAD] * ext_ref[0]
        edge_y = pairs_ref[j, t * TERM_PAD] * ext_ref[1]
        for k in range(1, terms):
            factor = pairs_ref[j, t * TERM_PAD + k]
            edge_x = edge_x + factor * ext_ref[2 * k]
            edge_y = edge_y + factor * ext_ref[2 * k + 1]
        return edge_x, edge_y

    lines = []
    for g in range(groups):
        edges = coef(g, g)
        basis = krylov(ext_ref[2 * terms + g], edges, scale_in, masks)
        for i, v in enumerate(basis):
            basis_ref[g * INNER + i] = v
        lines += moments_of(basis, edges, scale_in, diagonal, masks, rows)
    scatter(moments_ref, lines)

    def keep(at, t, j):
        edge_x, edge_y = coef(t, j)
        edges_ref[2 * at] = edge_x
        edges_ref[2 * at + 1] = edge_y

    at = 0
    for g in range(groups):
        resid_ref[g] = ext_ref[2 * terms + groups + g]
        keep(at, groups + g, groups + g)
        at += 1
        for j in range(groups):
            keep(at, groups + g, j)
            at += 1
    final = 2 * groups + rank
    resid_ref[groups] = ext_ref[2 * terms + final]
    keep(at, final, final)
    at += 1
    for j in range(2 * groups):
        keep(at, final, j)
        at += 1


def repeat(count, small, body):
    if small:
        for i in range(count):
            body(i)
    else:
        lax.fori_loop(0, count, lambda i, carry: (body(i), carry)[1], 0)


def second_kernel(dims, arrived_ref, basis_ref, resid_ref, edges_ref, diag_ref,
                  moments_ref, next_ref, tower_ref, heavy_ref, lines_ref):
    groups, count, rows, cols, terms, targets = dims
    size = rows + 2 * EDGE
    masks = lane_masks(size, cols)
    mine = slice(EDGE, EDGE + rows)
    total = gather(arrived_ref)
    updates = []
    for g in range(groups):
        mu = [total[g * 2 * INNER + m : g * 2 * INNER + m + 1] for m in range(2 * INNER)]
        updates.append(combine([basis_ref[g * INNER + i] for i in range(INNER)], coefficients(mu)))
        next_ref[groups * INNER + g] = updates[g][mine]
    scale_in = (diag_ref[1], SCALE * diag_ref[1])
    weight = diag_ref[0][mine]
    final = groups * (1 + groups)
    seeds = 1 + groups * INNER
    lines_ref[...] = jnp.zeros_like(lines_ref)

    def across(field, at):
        return apply_edges(field, edges_ref[2 * at], edges_ref[2 * at + 1], masks)

    def grow(seed, p):
        basis = krylov(seed, (edges_ref[2 * final], edges_ref[2 * final + 1]), scale_in, masks)
        basis.append(scale_in[1] * across(basis[-1], final) - SCALE * basis[-1])
        for i, v in enumerate(basis):
            tower_ref[i * seeds + p] = v[mine]
            if i < INNER:
                heavy_ref[i * seeds + p] = v[mine] * weight

    seed = resid_ref[groups]
    for j in range(groups):
        seed = seed - across(updates[j], final + 1 + j)
    grow(seed, 0)
    at = 0
    for g in range(groups):
        edges = (edges_ref[2 * at], edges_ref[2 * at + 1])
        at += 1
        residual = resid_ref[g]
        for j in range(groups):
            residual = residual - across(updates[j], at)
            at += 1
        basis = krylov(residual, edges, scale_in, masks)
        for i, v in enumerate(basis):
            next_ref[g * INNER + i] = v[mine]
            grow(across(v, final + 1 + groups + g), 1 + g * INNER + i)
        for m, line in enumerate(moments_of(basis, edges, scale_in, diag_ref[0], masks, rows)):
            lines_ref[g * 2 * INNER + m : g * 2 * INNER + m + 1, :] = line
    head, stride = pair_layout(groups)

    def one_moment(m):
        at = 0
        for p in range(seeds):
            for q in range(p, seeds):
                product = heavy_ref[(m // 2) * seeds + p] * tower_ref[((m + 1) // 2) * seeds + q]
                lines_ref[pl.ds(head + m * stride + at, 1), :] = jnp.sum(product, axis=0, keepdims=True)
                at += 1

    repeat(2 * INNER, groups <= 2, one_moment)
    packed = dot(jnp.ones((8, cols), F32), lines_ref[...], ((1,), (1,)))
    moments_ref[...] = jnp.zeros_like(moments_ref)
    for j in range(packed.shape[1] // cols):
        for d in range(moments_ref.shape[0]):
            moments_ref[d, j : j + 1, :] = packed[0:1, j * cols : (j + 1) * cols]


def pair_layout(groups):
    seeds = 1 + groups * INNER
    return round_up(groups * 2 * INNER, 8), round_up(seeds * (seeds + 1) // 2, 8)


def last_kernel(dims, order_ref, arrived_ref, basis_ref, tower_ref, start_ref, out_ref, lines_ref, pair_ref):
    groups, count, rows, cols, terms, targets = dims
    rank = lax.axis_index("chaos")
    packed = jnp.sum(arrived_ref[...], axis=0)
    ones = jnp.ones((cols, cols), F32)
    eye = lax.broadcasted_iota(jnp.int32, (cols, cols), 0) == lax.broadcasted_iota(jnp.int32, (cols, cols), 1)
    for j in range(lines_ref.shape[0] // cols):
        spread = jnp.where(eye, packed[j : j + 1, :], 0.0)
        lines_ref[j * cols : (j + 1) * cols, :] = dot(spread, ones, ((1,), (0,)))
    seeds = 1 + groups * INNER
    weights = [jnp.ones((1, cols), F32)]
    updates = []
    for g in range(groups):
        first = g * 2 * INNER
        parts = coefficients([lines_ref[first + m : first + m + 1, :] for m in range(2 * INNER)])
        updates.append(parts)
        weights += [-part for part in parts]
    head, stride = pair_layout(groups)
    pair_ref[...] = jnp.zeros_like(pair_ref)
    at = 0
    for p in range(seeds):
        for q in range(p, seeds):
            pair_ref[at : at + 1, :] = weights[p] * weights[q] * (1.0 if p == q else 2.0)
            at += 1
    pairs = pair_ref[...]
    mu = [
        jnp.sum(pairs * lines_ref[head + m * stride : head + (m + 1) * stride, :], axis=0, keepdims=True)
        for m in range(2 * INNER)
    ]
    parts = coefficients(mu)
    third = None
    for i in range(INNER):
        level = combine([tower_ref[i * seeds + p] for p in range(seeds)], weights)
        third = parts[i] * level if third is None else third + parts[i] * level
    own = [updates[0][i] for i in range(INNER)]
    for g in range(1, groups):
        own = [jnp.where(rank == g, updates[g][i], own[i]) for i in range(INNER)]
    second = combine([basis_ref[rank * INNER + i] for i in range(INNER)], own)
    slots = slots_of(order_ref, rank * count, count)
    out_ref[...] = start_ref[...]
    out_ref[slots[0]] = out_ref[slots[0]] + basis_ref[groups * INNER + rank]
    out_ref[slots[1]] = out_ref[slots[1]] + second
    out_ref[slots[2]] = out_ref[slots[2]] + third


def on_device(rhs, start, kl_fields, coupling, order):
    count, rows, cols = start.shape
    terms = kl_fields.shape[0]
    groups = lax.axis_size("chaos")
    spaces = lax.axis_size("space")
    targets = SECTIONS * groups
    dims = (groups, count, rows, cols, terms, targets)
    tall = TERM_PAD * targets
    size = rows + 2 * EDGE
    wide = round_up(tall, 128)
    vmem = pl.BlockSpec(memory_space=pltpu.VMEM)
    smem = pl.BlockSpec(memory_space=pltpu.SMEM)

    def call(body, specs, outs, scratch=()):
        return pl.pallas_call(
            lambda *refs: body(dims, *refs),
            out_shape=[jax.ShapeDtypeStruct(s, F32) for s in outs],
            in_specs=specs,
            out_specs=[vmem] * len(outs),
            scratch_shapes=[pltpu.VMEM(s, F32) for s in scratch],
            name=body.__name__,
        )

    flat_start = start.reshape(count * rows, cols)
    flat_kl = kl_fields.reshape(2 * terms * rows, cols)
    pay_rows = targets * rows + 2 * tall
    pay, pairs = call(
        base_kernel, [smem, vmem, vmem, vmem, vmem],
        [(pay_rows, cols), (round_up(targets, 8), wide)],
        [(wide, coupling.shape[1]), (tall * rows, cols)],
    )(order, coupling, flat_start, rhs, flat_kl)

    def swap(array, bit):
        return lax.ppermute(array, "chaos", [(i, i ^ bit) for i in range(groups)])

    bit = groups // 2
    while bit > 1:
        pay = pay + swap(pay, bit)
        bit //= 2
    other = swap(pay, 1)
    halo_rows = round_up((2 * terms + targets) * HALO + tall, 8)
    full, halo = call(
        pack_kernel, [vmem] * 3, [(pay_rows, cols), (halo_rows, cols)]
    )(pay, other, flat_kl)
    pairs_list = []
    for c in range(groups):
        step = 1 if c % 2 == 0 else -1
        for i in range(spaces):
            if 0 <= i + step < spaces:
                pairs_list.append((c * spaces + i, c * spaces + i + step))
    got = lax.ppermute(halo, ("chaos", "space"), pairs_list)
    swapped = swap(got, 1)
    couples = groups * (1 + groups) + 1 + 2 * groups
    moment_rows = round_up(groups * 2 * INNER, 8)
    moments, basis, resid, edges, diag = call(
        first_kernel, [smem, vmem, vmem, vmem, vmem],
        [(spaces, moment_rows, cols), (groups * INNER, size, cols), (groups + 1, size, cols),
         (2 * couples, size, cols), (2, size, cols)],
        [(2 * terms + targets, size, cols), (2, tall, cols)],
    )(pairs, full, flat_kl, got, swapped)

    def share(array):
        return lax.all_to_all(array, "space", 0, 0, tiled=True)

    seeds = 1 + groups * INNER
    head, stride = pair_layout(groups)
    lines = round_up(head + 2 * INNER * stride, cols)
    moments, basis, tower = call(
        second_kernel, [vmem] * 5,
        [(spaces, round_up(lines // cols, 8), cols), (groups * (INNER + 1), rows, cols), ((INNER + 1) * seeds, rows, cols)],
        [(INNER * seeds, rows, cols), (lines, cols)],
    )(share(moments), basis, resid, edges, diag)
    (out,) = call(
        last_kernel, [smem] + [vmem] * 4, [(count, rows, cols)], [(lines, cols), (stride, cols)]
    )(order, share(moments), basis, tower, start)
    return out


def solution(mesh):
    return jax.shard_map(
        on_device,
        mesh=mesh,
        in_specs=(
            P("chaos", "space", None),
            P("chaos", "space", None),
            P(None, None, "space", None),
            P(),
            P(),
        ),
        out_specs=P("chaos", "space", None),
        check_vma=False,
    )
```
